32 devices in a mesh: dp: 8 (over z, x), seq: 4 (over y, core).
Axes of the slice: x: 2, y: 2, z: 4, core: 2. Of those that a mesh axis runs over, the one named last changes fastest.
Arguments:
- block_input: bfloat16 [8, 512, 1024], P('dp', 'seq'), may hold values from -6 to 6
- out_grad: bfloat16 [8, 512, 1024], P('dp', 'seq'), may hold values from -6 to 6
- segments: int32 [8, 512], P('dp'), may hold values from 0 to 3, never falling along the last dimension, each value on 1 to 256 neighbouring positions
- routes: int32 [8, 512, 8], P('dp', 'seq'), may hold values from 0 to 31, all different within a row; in each aligned block of 128 rows (0 to 127, 128 to 255, ..., all dimensions but the last counted through in order) at most 34 rows name the same one
- gain_attn: bfloat16 [1024], P(('dp', 'seq')), may hold values from 0.5 to 1.5
- w_qkv: bfloat16 [1024, 2048], P(('dp', 'seq')), may hold values from -0.1875 to 0.1875
- w_out: bfloat16 [1024, 1024], P(('dp', 'seq')), may hold values from -2 to 2
- gain_moe: bfloat16 [1024], P(('dp', 'seq')), may hold values from 0.5 to 1.5
- router: bfloat16 [1024, 32], P(('dp', 'seq')), may hold values from -0.1875 to 0.1875
- w_in: bfloat16 [32, 1024, 1024], P('dp', 'seq'), may hold values from -0.1875 to 0.1875
- w_down: bfloat16 [32, 512, 1024], P('dp', None, 'seq'), may hold values from -0.75 to 0.75
Outputs:
- block_output: bfloat16 [8, 512, 1024], P('dp', 'seq')
- input_grad: float32 [8, 512, 1024], P('dp', 'seq')
- gain_attn_grad: float32 [1024], P(('dp', 'seq'))
- w_qkv_grad: float32 [1024, 2048], P(('dp', 'seq'))
- w_out_grad: float32 [1024, 1024], P(('dp', 'seq'))
- gain_moe_grad: float32 [1024], P(('dp', 'seq'))
- router_grad: float32 [1024, 32], P(('dp', 'seq'))
- w_in_grad: float32 [32, 1024, 1024], P('dp', 'seq')
- w_down_grad: float32 [32, 512, 1024], P('dp', None, 'seq')
The draws below stay inside these ranges and needn't reach their ends.
Inputs may be any that keep to these rules, and one draw needn't show every extreme that they name: `routes`: within the 128 rows of one device no expert is named by more than 34 rows, and in some device's rows one expert is named by exactly 34. `segments`: segment numbers never fall along a packed sequence.
All inputs are finite; a program needn't handle non-finite values.
Results may differ from the reference program's by a relative error of at most 0.015.
Values may be sent and summed in bfloat16 or wider, within the bound.
A program may use at most 128 MiB of HBM per device.

```python
import math
import jax
import jax.numpy as jnp
import numpy as np
from jax import lax

D = 1024
HEADS = 16
KV_HEADS = 8
HEAD_DIM = 64
EXPERTS = 32
FF = 512
TOP = 8
TOK_DEV = 128
LENGTH = 512
NSEQ = 8
HH = 1024
QKV = 2048
CAP = 34


def block_scale(rng, shape, pieces, smallest, high):
    def one(dim, parts):
        draws = jax.random.uniform(jax.random.fold_in(jax.random.fold_in(rng, 6), dim), (parts,), jnp.float32, smallest / len(pieces), high / len(pieces))
        return jnp.repeat(jnp.exp(draws), shape[dim] // parts).reshape((-1,) + (1,) * (len(shape) - dim - 1))

    factor_of = one(*pieces[0])
    for cut in pieces[1:]:
        factor_of = factor_of * one(*cut)
    return factor_of


def length_profile(amount, total, limit, slope):
    loads = [(1 << 20) // math.isqrt(grade ** slope) + 1 for grade in range(2, amount + 1)]
    rest, holding = total - limit - (amount - 1), [1] * (amount - 1)
    while rest > 0:
        movable = [i for i in range(amount - 1) if holding[i] < limit]
        whole, left = sum([loads[i] for i in movable]), rest
        for i in movable:
            extra = min(limit - holding[i], max(1, left * loads[i] // whole), rest)
            holding[i] = holding[i] + extra
            rest = rest - extra
    return np.array([limit] + holding)


def uneven_parts(rng, amount, total, bound, skew):
    if amount == 2:
        one = jax.random.randint(rng, (), max(1, total - bound), min(bound, total - 1) + 1)
        return jnp.stack([one, total - one])
    sizes = jnp.asarray(length_profile(amount, total, bound, skew), jnp.int32)
    couples = (amount - 1) // 2
    source_of, receiver = sizes[1:1 + 2 * couples:2], sizes[2:2 + 2 * couples:2]
    room = jnp.minimum(source_of - 1, bound - receiver)
    shifted = jax.random.randint(jax.random.fold_in(rng, 1), (couples,), 0, 1 << 20) % (room + 1)
    sizes = sizes.at[1:1 + 2 * couples:2].set(source_of - shifted).at[2:2 + 2 * couples:2].set(receiver + shifted)
    return sizes[jax.random.permutation(jax.random.fold_in(rng, 2), amount)]


def deal_out(key, own, number, rows, amount, top, most, skew):
    order = jax.random.permutation(key, amount)
    crowded, usual = shares(amount, rows * top, most, skew, True), shares(amount, rows * top, most, skew, False)
    places = jnp.arange(amount)

    def named(tallies, turn):
        used = int((tallies > 0).sum())
        fixed = max(1, used // 4)
        passed = fixed + (places - fixed + turn * (used - fixed)) % max(1, amount - fixed)
        return jnp.zeros((amount,), jnp.int32).at[order[jnp.where(places < fixed, places, passed)]].set(jnp.asarray(tallies, jnp.int32))

    tallies = jnp.where(number % 4 == 0, named(crowded, number // 4), named(usual, number - number // 4 - 1))
    mixed = jax.random.permutation(jax.random.fold_in(own, 3), amount)
    giver, taker = mixed[0:amount // 2 * 2:2], mixed[1:amount // 2 * 2:2]
    margin = jnp.minimum(tallies[giver] - 1, most - tallies[taker]) // 2
    margin = jnp.where((giver == order[0]) | (taker == order[0]) | (tallies[taker] == 0), 0, jnp.maximum(margin, 0))
    passed = jax.random.randint(jax.random.fold_in(own, 4), (amount // 2,), 0, 1 << 20) % (margin + 1)
    tallies = tallies.at[giver].add(-passed).at[taker].add(passed)
    items = jnp.searchsorted(jnp.cumsum(tallies), jnp.arange(rows * top), side="right").astype(jnp.int32)
    grid = items.reshape(top, rows).T
    grid = grid[jax.random.permutation(jax.random.fold_in(own, 1), rows)]
    turn = jax.random.randint(jax.random.fold_in(own, 2), (rows, 1), 0, top)
    return jnp.take_along_axis(grid, (jnp.arange(top)[None, :] + turn) % top, axis=1)


def shares(count, total, bound, lean, full):
    portions = [(1 << 20) // math.isqrt(rank ** lean) + 1 for rank in range(1, count + 1)]
    largest = bound if full else min(bound, max(-(-total // count), total * portions[0] // sum(portions)))
    least = 1 if total - largest >= count - 1 else 0
    holding, rest = [largest] + [least] * (count - 1), total - largest - least * (count - 1)
    while rest > 0:
        candidates = [i for i in range(1, count) if holding[i] < largest] or [i for i in range(1, count) if holding[i] < bound]
        mass, remaining = sum([portions[i] for i in candidates]), rest
        for i in candidates:
            more = min(bound - holding[i], max(1, remaining * portions[i] // mass), rest)
            holding[i] = holding[i] + more
            rest = rest - more
    return np.array(holding)


def gaussian(stream_key, dims, scale, limit, cuts=(), kind=jnp.bfloat16):
    result = jax.random.normal(stream_key, dims, jnp.float32) * scale
    if len(cuts) > 0:
        result = block_scale(stream_key, dims, cuts, -0.22, 0.18) * result
    return jnp.clip(result, min=-limit, max=limit).astype(kind)


def setup_inputs(seed: int = 0) -> dict:
    key_list = jax.random.split(jax.random.key(seed), 12)
    block_input = gaussian(key_list[0], (NSEQ, LENGTH, D), 1.0, 6.0, ((0, 8), (1, 4)))
    out_grad = gaussian(key_list[1], (NSEQ, LENGTH, D), 1.0, 6.0, ((0, 8), (1, 4)))
    segments = jax.vmap(lambda own: jnp.searchsorted(jnp.cumsum(uneven_parts(own, max(4, LENGTH // 256), LENGTH, LENGTH // 2, 0)), jnp.arange(LENGTH), side="right"))(jax.random.split(key_list[2], NSEQ)).reshape((NSEQ, LENGTH)).astype(jnp.int32)
    routes_keys = jax.random.split(jax.random.fold_in(key_list[3], 1), NSEQ * LENGTH // TOK_DEV)
    routes_turns = jax.random.permutation(jax.random.fold_in(key_list[3], 3), NSEQ * LENGTH // TOK_DEV)
    routes = jax.vmap(lambda own, number: deal_out(jax.random.fold_in(key_list[3], 2), own, number, TOK_DEV, EXPERTS, TOP, CAP, 1))(routes_keys, routes_turns).reshape((NSEQ, LENGTH, TOP))
    gain_attn = jnp.clip(1.0 + 0.1 * jax.random.normal(key_list[4], (D,), jnp.float32), 0.5, 1.5).astype(jnp.bfloat16)
    w_qkv = gaussian(key_list[5], (D, QKV), D ** -0.5, 0.1875, ((0, 32),))
    w_out = gaussian(key_list[6], (HH, D), (HH // 128) ** -0.5, 2.0, ((0, 32),))
    gain_moe = jnp.clip(1.0 + 0.1 * jax.random.normal(key_list[7], (D,), jnp.float32), 0.5, 1.5).astype(jnp.bfloat16)
    router = gaussian(key_list[8], (D, EXPERTS), D ** -0.5, 0.1875, ((0, 32),))
    w_in = gaussian(key_list[9], (EXPERTS, D, 2 * FF), D ** -0.5, 0.1875, ((0, 8), (1, 4)))
    w_down = gaussian(key_list[10], (EXPERTS, FF, D), (FF // 8) ** -0.5, 0.75, ((0, 8), (2, 4)))
    return dict(block_input=block_input, out_grad=out_grad, segments=segments, routes=routes, gain_attn=gain_attn, w_qkv=w_qkv, w_out=w_out, gain_moe=gain_moe, router=router, w_in=w_in, w_down=w_down)


epsilon = 1e-05
score_scale = 0.125
masked_score = -1e+30
theta_base = 10000.0

def narrow(values):
    return lax.optimization_barrier(values.astype(jnp.bfloat16))

def inverse_root(values):
    return lax.rsqrt(lax.optimization_barrier(jnp.mean(values * values, axis=-1, keepdims=True)) + epsilon)

def rope_tables(positions):
    half_dim = HEAD_DIM // 2
    frequencies = theta_base ** (-2.0 * jnp.arange(half_dim, dtype=jnp.float32) / HEAD_DIM)
    angles = positions.astype(jnp.float32)[:, None] * frequencies[None, :]
    return (jnp.cos(angles)[:, None, :], jnp.sin(angles)[:, None, :])

def rotate(values, cosine_table, sine_table):
    half_dim = HEAD_DIM // 2
    first_half = values[..., :half_dim]
    second_half = values[..., half_dim:]
    return jnp.concatenate([first_half * cosine_table - second_half * sine_table, second_half * cosine_table + first_half * sine_table], axis=-1)

def unrotate(values, cosine_table, sine_table):
    half_dim = HEAD_DIM // 2
    first_half = values[..., :half_dim]
    second_half = values[..., half_dim:]
    return jnp.concatenate([first_half * cosine_table + second_half * sine_table, second_half * cosine_table - first_half * sine_table], axis=-1)

def doc_positions(query_segs, all_segs, first_index):
    earlier = lax.optimization_barrier(jnp.sum((all_segs[None, :] < query_segs[:, None]).astype(jnp.int32), axis=1)).astype(jnp.int32)
    return first_index + jnp.arange(query_segs.shape[0], dtype=jnp.int32) - earlier

def slot_index(block_routes):
    onehot = (block_routes[..., None] == jnp.arange(EXPERTS, dtype=jnp.int32)).astype(jnp.int32).reshape(-1, EXPERTS)
    running = jnp.cumsum(onehot, axis=0).astype(jnp.int32)
    slot_rank = lax.optimization_barrier(jnp.sum(running * onehot, axis=1)).astype(jnp.int32) - 1
    return (block_routes.reshape(-1) * CAP + slot_rank).astype(jnp.int32)

def reference(block_input, out_grad, segments, routes, gain_attn, w_qkv, w_out, gain_moe, router, w_in, w_down):
    heads_width = HEADS * HEAD_DIM
    kv_width = KV_HEADS * HEAD_DIM
    groups = HEADS // KV_HEADS
    length = block_input.shape[1]
    blocks = length // TOK_DEV
    model_width = block_input.shape[2]
    w_in_wide = w_in.astype(jnp.float32)
    w_down_wide = w_down.astype(jnp.float32)
    gain_one = gain_attn.astype(jnp.float32)
    gain_two = gain_moe.astype(jnp.float32)
    router_wide = router.astype(jnp.float32)
    expert_ids = jnp.arange(EXPERTS, dtype=jnp.int32)
    key_index = jnp.arange(length, dtype=jnp.int32)

    def place_rows(index_row, value_rows):
        return jnp.zeros((EXPERTS * CAP, model_width), jnp.bfloat16).at[index_row].set(value_rows)

    def to_experts(token_rows, indices):
        placed = jax.vmap(place_rows)(indices, token_rows)
        return placed.reshape(blocks, EXPERTS, CAP, model_width).transpose(1, 0, 2, 3).reshape(EXPERTS, blocks * CAP, model_width)

    def from_experts(expert_rows, indices):
        by_source = expert_rows.reshape(EXPERTS, blocks, CAP, model_width).transpose(1, 0, 2, 3).reshape(blocks, EXPERTS * CAP, model_width)
        picked_rows = jax.vmap(lambda rows_in, index_row: rows_in[index_row])(by_source, indices)
        return picked_rows.reshape(length, TOP, model_width)

    def one_sequence(totals, inputs):
        tokens, cotangent, seg_ids, seq_routes = inputs
        input_wide = tokens.astype(jnp.float32)
        root_one = inverse_root(input_wide)
        normed_one = input_wide * root_one
        attn_in = narrow(normed_one * gain_one)
        projected = jnp.dot(attn_in, w_qkv, preferred_element_type=jnp.float32)
        positions = doc_positions(seg_ids, seg_ids, 0)
        cosine_table, sine_table = rope_tables(positions)
        queries = narrow(rotate(projected[:, :heads_width].reshape(length, HEADS, HEAD_DIM), cosine_table, sine_table))
        key_rows = narrow(rotate(projected[:, heads_width:heads_width + kv_width].reshape(length, KV_HEADS, HEAD_DIM), cosine_table, sine_table))
        value_rows = narrow(projected[:, heads_width + kv_width:].reshape(length, KV_HEADS, HEAD_DIM))
        grouped = queries.astype(jnp.float32).reshape(length, KV_HEADS, groups, HEAD_DIM)
        keys_wide = key_rows.astype(jnp.float32)
        values_wide = value_rows.astype(jnp.float32)
        allowed = (key_index[None, :] <= key_index[:, None]) & (seg_ids[None, :] == seg_ids[:, None])
        scores = jnp.einsum('tkgd,skd->kgts', grouped, keys_wide) * score_scale
        scores = jnp.where(allowed, scores, masked_score)
        top_score = lax.optimization_barrier(jnp.max(scores, axis=-1, keepdims=True))
        log_total = top_score + jnp.log(lax.optimization_barrier(jnp.sum(jnp.exp(scores - top_score), axis=-1, keepdims=True)))
        attn_probs = jnp.exp(scores - log_total)
        probs_low = narrow(attn_probs).astype(jnp.float32)
        attn_mix = narrow(jnp.einsum('kgts,skd->tkgd', probs_low, values_wide).reshape(length, heads_width))
        state = input_wide + jnp.dot(attn_mix, w_out, preferred_element_type=jnp.float32)
        root_two = inverse_root(state)
        normed_two = state * root_two
        moe_in = narrow(normed_two * gain_two)
        logits = jnp.dot(moe_in, router, preferred_element_type=jnp.float32)
        choose = (seq_routes[..., None] == expert_ids).astype(jnp.float32)
        picked = lax.optimization_barrier(jnp.sum(choose * logits[:, None, :], axis=-1))
        route_weights = jax.nn.softmax(picked, axis=-1)
        indices = jax.vmap(slot_index)(seq_routes.reshape(blocks, TOK_DEV, TOP))
        spread = jnp.broadcast_to(moe_in[:, None, :], (length, TOP, model_width)).reshape(blocks, TOK_DEV * TOP, model_width)
        rows_wide = to_experts(spread, indices).astype(jnp.float32)
        gate_up = jnp.einsum('ecd,edf->ecf', rows_wide, w_in_wide)
        gate_part = gate_up[..., :FF]
        up_part = gate_up[..., FF:]
        sigmoid_gate = jax.nn.sigmoid(gate_part)
        activated = narrow(gate_part * sigmoid_gate * up_part).astype(jnp.float32)
        expert_out = narrow(jnp.einsum('ecf,efd->ecd', activated, w_down_wide))
        token_out = from_experts(expert_out, indices).astype(jnp.float32)
        output = (state + lax.optimization_barrier(jnp.sum(route_weights[..., None] * token_out, axis=1))).astype(jnp.bfloat16)
        out_wide = cotangent.astype(jnp.float32)
        weight_grad = lax.optimization_barrier(jnp.sum(out_wide[:, None, :] * token_out, axis=-1))
        routed_grad = narrow(route_weights[..., None] * out_wide[:, None, :])
        grad_rows = to_experts(routed_grad.reshape(blocks, TOK_DEV * TOP, model_width), indices).astype(jnp.float32)
        act_grad = jnp.einsum('ecd,efd->ecf', grad_rows, w_down_wide)
        down_total = jnp.einsum('ecf,ecd->efd', activated, grad_rows)
        gate_grad = act_grad * up_part * sigmoid_gate * (1.0 + gate_part * (1.0 - sigmoid_gate))
        up_grad = act_grad * gate_part * sigmoid_gate
        gate_up_grad = narrow(jnp.concatenate([gate_grad, up_grad], axis=-1)).astype(jnp.float32)
        in_total = jnp.einsum('ecd,ecf->edf', rows_wide, gate_up_grad)
        rows_grad = narrow(jnp.einsum('ecf,edf->ecd', gate_up_grad, w_in_wide))
        moe_in_grad = lax.optimization_barrier(jnp.sum(from_experts(rows_grad, indices).astype(jnp.float32), axis=1))
        picked_grad = route_weights * (weight_grad - lax.optimization_barrier(jnp.sum(route_weights * weight_grad, axis=-1, keepdims=True)))
        logit_grad = lax.optimization_barrier(jnp.sum(picked_grad[..., None] * choose, axis=1))
        router_total = jnp.dot(moe_in.astype(jnp.float32).T, logit_grad, precision=lax.Precision.HIGHEST)
        moe_in_grad = moe_in_grad + jnp.dot(logit_grad, router_wide.T, precision=lax.Precision.HIGHEST)
        gain_two_total = lax.optimization_barrier(jnp.sum(moe_in_grad * normed_two, axis=0))
        normed_two_grad = moe_in_grad * gain_two
        state_grad = out_wide + root_two * (normed_two_grad - normed_two * lax.optimization_barrier(jnp.mean(normed_two_grad * normed_two, axis=-1, keepdims=True)))
        state_low = narrow(state_grad)
        out_total = jnp.dot(attn_mix.T, state_low, preferred_element_type=jnp.float32)
        mix_grad = narrow(jnp.dot(state_low, w_out.T, preferred_element_type=jnp.float32)).astype(jnp.float32).reshape(length, KV_HEADS, groups, HEAD_DIM)
        raw_grad = jnp.einsum('tkgd,skd->kgts', mix_grad, values_wide)
        row_delta = lax.optimization_barrier(jnp.sum(mix_grad * attn_mix.astype(jnp.float32).reshape(length, KV_HEADS, groups, HEAD_DIM), axis=-1))
        row_delta = jnp.transpose(row_delta, (1, 2, 0))[..., None]
        scores_grad = narrow(attn_probs * (raw_grad - row_delta) * score_scale).astype(jnp.float32)
        query_grad = jnp.einsum('kgts,skd->tkgd', scores_grad, keys_wide).reshape(length, HEADS, HEAD_DIM)
        key_grad = jnp.einsum('kgts,tkgd->skd', scores_grad, grouped)
        value_grad = jnp.einsum('kgts,tkgd->skd', probs_low, mix_grad)
        query_grad = unrotate(query_grad, cosine_table, sine_table)
        key_grad = unrotate(key_grad, cosine_table, sine_table)
        proj_grad = narrow(jnp.concatenate([query_grad.reshape(length, heads_width), key_grad.reshape(length, kv_width), value_grad.reshape(length, kv_width)], axis=-1))
        qkv_total = jnp.dot(attn_in.T, proj_grad, preferred_element_type=jnp.float32)
        attn_in_grad = jnp.dot(proj_grad, w_qkv.T, preferred_element_type=jnp.float32)
        gain_one_total = lax.optimization_barrier(jnp.sum(attn_in_grad * normed_one, axis=0))
        normed_one_grad = attn_in_grad * gain_one
        input_grad = state_grad + root_one * (normed_one_grad - normed_one * lax.optimization_barrier(jnp.mean(normed_one_grad * normed_one, axis=-1, keepdims=True)))
        new_totals = (totals[0] + gain_one_total, totals[1] + qkv_total, totals[2] + out_total, totals[3] + gain_two_total, totals[4] + router_total, totals[5] + in_total, totals[6] + down_total)
        return (new_totals, (output, input_grad))
    start_totals = (jnp.zeros(gain_attn.shape, jnp.float32), jnp.zeros(w_qkv.shape, jnp.float32), jnp.zeros(w_out.shape, jnp.float32), jnp.zeros(gain_moe.shape, jnp.float32), jnp.zeros(router.shape, jnp.float32), jnp.zeros(w_in.shape, jnp.float32), jnp.zeros(w_down.shape, jnp.float32))
    totals, results = lax.scan(one_sequence, start_totals, (block_input, out_grad, segments, routes))
    return (results[0], results[1], totals[0], totals[1], totals[2], totals[3], totals[4], totals[5], totals[6])
```

```python
import jax
import jax.numpy as jnp
from jax import lax
from jax.sharding import PartitionSpec as P

HEADS = 16
KV_HEADS = 8
HEAD_DIM = 64
EXPERTS = 32
FF = 512
TOP = 8
CAP = 34


epsilon = 1e-05
score_scale = 0.125
masked_score = -1e30
theta_base = 10000.0


def inverse_root(values):
    return lax.rsqrt(jnp.mean(values * values, axis=-1, keepdims=True) + epsilon)


def rope_tables(positions):
    half_dim = HEAD_DIM // 2
    frequencies = theta_base ** (-2.0 * jnp.arange(half_dim, dtype=jnp.float32) / HEAD_DIM)
    angles = positions.astype(jnp.float32)[:, None] * frequencies[None, :]
    return (jnp.cos(angles)[:, None, :], jnp.sin(angles)[:, None, :])


def rotate(values, cosine_table, sine_table):
    half_dim = HEAD_DIM // 2
    first_half = values[..., :half_dim]
    second_half = values[..., half_dim:]
    return jnp.concatenate(
        [
            first_half * cosine_table - second_half * sine_table,
            second_half * cosine_table + first_half * sine_table,
        ],
        axis=-1,
    )


def unrotate(values, cosine_table, sine_table):
    half_dim = HEAD_DIM // 2
    first_half = values[..., :half_dim]
    second_half = values[..., half_dim:]
    return jnp.concatenate(
        [
            first_half * cosine_table + second_half * sine_table,
            second_half * cosine_table - first_half * sine_table,
        ],
        axis=-1,
    )


def doc_positions(query_segs, all_segs, first_index):
    earlier = jnp.sum((all_segs[None, :] < query_segs[:, None]).astype(jnp.int32), axis=1)
    return first_index + jnp.arange(query_segs.shape[0], dtype=jnp.int32) - earlier


def swap(values, axis, bit):
    size = lax.axis_size(axis)
    return lax.ppermute(values, axis, [(i, i ^ bit) for i in range(size)])


def axis_bits(axis):
    bits = []
    bit = 1
    while bit < lax.axis_size(axis):
        bits.append(bit)
        bit *= 2
    return bits


def gather_shards(shard, axis, dim):
    index = lax.axis_index(axis)
    bits = axis_bits(axis)
    pieces = {0: shard}
    for bit in bits[1:] + bits[:1]:
        mine_high = (index & bit) != 0
        grown = {}
        for place, piece in pieces.items():
            other = swap(piece, axis, bit)
            grown[place] = jnp.where(mine_high, other, piece)
            grown[place | bit] = jnp.where(mine_high, piece, other)
        pieces = grown
    return jnp.concatenate([pieces[i] for i in range(len(pieces))], axis=dim)


def reduce_shards(partial, stages, dims):
    value = partial
    sizes = {axis: axis_bits(axis) for axis in dims}
    for number, (axis, bit) in enumerate(stages):
        dim = dims[axis]
        left = sizes[axis]
        at = left.index(bit)
        high = 2 ** (len(left) - 1 - at)
        low = 2**at
        shape = value.shape
        split = value.reshape(shape[:dim] + (high, 2, low) + shape[dim + 1 :])
        mine = jnp.where((lax.axis_index(axis) & bit) != 0, 1, 0)
        keep = lax.dynamic_index_in_dim(split, mine, dim + 1, keepdims=False)
        send = lax.dynamic_index_in_dim(split, 1 - mine, dim + 1, keepdims=False)
        got = swap(send.astype(jnp.bfloat16), axis, bit)
        value = keep.astype(jnp.float32) + got.astype(jnp.float32)
        value = value.reshape(shape[:dim] + (high * low,) + shape[dim + 1 :])
        sizes[axis] = left[:at] + left[at + 1 :]
        if number + 1 < len(stages):
            value = value.astype(jnp.bfloat16)
    return value


def expert_weights(logits, chosen):
    top = jnp.max(jnp.where(chosen, logits, -jnp.inf), axis=-1, keepdims=True)
    raised = jnp.where(chosen, jnp.exp(jnp.where(chosen, logits - top, 0.0)), 0.0)
    return raised / jnp.sum(raised, axis=-1, keepdims=True)


def pad_columns(arrays, width):
    rows = arrays[0].shape[0]
    used = sum(a.shape[1] for a in arrays)
    return jnp.concatenate(
        list(arrays) + [jnp.zeros((rows, width - used), arrays[0].dtype)], axis=1
    )


def body(
    block_input, out_grad, segments, routes, gain_attn, w_qkv, w_out, gain_moe, router, w_in, w_down
):
    tokens = block_input[0]
    cotangent = out_grad[0]
    seg_ids = segments[0]
    tok_routes = routes[0]
    local_rows = tokens.shape[0]
    model_width = tokens.shape[1]
    length = seg_ids.shape[0]
    heads_width = HEADS * HEAD_DIM
    kv_width = KV_HEADS * HEAD_DIM
    groups = HEADS // KV_HEADS
    key_block = min(length, 256)
    first_row = lax.axis_index("seq") * local_rows
    qkv_width = w_qkv.shape[1]
    out_width = w_out.shape[1]
    dp_size = lax.axis_size("dp")
    dp_index = lax.axis_index("dp")
    owned = EXPERTS // dp_size
    rows_each = dp_size * CAP
    group_rows = dp_size * local_rows
    dp_bits = axis_bits("dp")
    seq_bits = axis_bits("seq")
    x_bits = dp_bits[:1]
    z_bits = dp_bits[:0:-1]
    first_dense = lax.all_gather(
        pad_columns([w_qkv, gain_attn[:, None]], qkv_width + 128),
        ("dp", "seq"), axis=0, tiled=True,
    )
    qkv_full = first_dense[:, :qkv_width]
    gain_full = first_dense[:, qkv_width]
    second_dense = lax.all_gather(
        pad_columns([w_out, router, gain_moe[:, None]], out_width + 128),
        ("dp", "seq"), axis=0, tiled=True,
    )
    out_full = second_dense[:, :out_width]
    router_full = second_dense[:, out_width : out_width + EXPERTS]
    gain_two_full = second_dense[:, out_width + EXPERTS]
    grads_group = lax.all_gather(
        pad_columns([cotangent, tok_routes.astype(jnp.bfloat16)], model_width + 128),
        "dp", axis=0, tiled=True,
    )
    routes_group = grads_group[:, model_width : model_width + TOP].astype(jnp.int32)
    grads_group = grads_group[:, :model_width]
    in_full = gather_shards(w_in, "seq", 1)
    down_full = gather_shards(w_down, "seq", 2)
    all_experts = jnp.arange(EXPERTS, dtype=jnp.int32)
    chosen_group = jnp.any(routes_group[:, :, None] == all_experts, axis=1)
    own_experts = dp_index * owned + jnp.arange(owned, dtype=jnp.int32)
    chosen_own = jnp.any(routes_group[None, :, :] == own_experts[:, None, None], axis=2)
    row_index = jnp.arange(group_rows, dtype=jnp.int32)
    upper = (row_index[:, None] <= row_index[None, :]).astype(jnp.bfloat16)
    slot_rank = (
        jnp.dot(chosen_own.astype(jnp.bfloat16), upper, preferred_element_type=jnp.float32)
        .astype(jnp.int32)
        - 1
    )
    slot_rank = jnp.where(chosen_own, slot_rank, -1)
    place = slot_rank[:, None, :] == jnp.arange(rows_each, dtype=jnp.int32)[None, :, None]
    place_low = place.astype(jnp.bfloat16).reshape(owned * rows_each, group_rows)
    input_wide = tokens.astype(jnp.float32)
    root_one = inverse_root(input_wide)
    normed_one = input_wide * root_one
    gain_one = gain_full.astype(jnp.float32)
    attn_in = (normed_one * gain_one).astype(jnp.bfloat16)
    projected = jnp.dot(attn_in, qkv_full, preferred_element_type=jnp.float32)
    query_segs = lax.dynamic_slice_in_dim(seg_ids, first_row, local_rows)
    positions = doc_positions(query_segs, seg_ids, first_row)
    cosine_table, sine_table = rope_tables(positions)
    queries = rotate(
        projected[:, :heads_width].reshape(local_rows, HEADS, HEAD_DIM), cosine_table, sine_table
    ).astype(jnp.bfloat16)
    key_local = (
        rotate(
            projected[:, heads_width : heads_width + kv_width].reshape(
                local_rows, KV_HEADS, HEAD_DIM
            ),
            cosine_table,
            sine_table,
        )
        .astype(jnp.bfloat16)
        .reshape(local_rows, kv_width)
    )
    value_local = projected[:, heads_width + kv_width :].astype(jnp.bfloat16)
    both_all = lax.all_gather(
        jnp.concatenate([key_local, value_local], axis=1), "seq", axis=0, tiled=True
    )
    key_all = both_all[:, :kv_width]
    value_all = both_all[:, kv_width:]
    grouped = queries.reshape(local_rows, KV_HEADS, groups, HEAD_DIM)
    query_index = first_row + jnp.arange(local_rows, dtype=jnp.int32)
    doc_start = jnp.sum((seg_ids < query_segs[0]).astype(jnp.int32))
    low_block = doc_start // key_block
    high_block = (first_row + local_rows - 1) // key_block + 1

    def block_keys(keys_flat, values_flat, number):
        start = (number * key_block).astype(jnp.int32)
        key_three = lax.dynamic_slice_in_dim(keys_flat, start, key_block, 0).reshape(
            key_block, KV_HEADS, HEAD_DIM
        )
        value_three = lax.dynamic_slice_in_dim(values_flat, start, key_block, 0).reshape(
            key_block, KV_HEADS, HEAD_DIM
        )
        return (start, key_three, value_three)

    def block_scores(start, key_three):
        raw_scores = (
            jnp.einsum("tkgd,skd->kgts", grouped, key_three, preferred_element_type=jnp.float32)
            * score_scale
        )
        block_index = start + jnp.arange(key_block, dtype=jnp.int32)
        block_segs = lax.dynamic_slice_in_dim(seg_ids, start, key_block)
        allowed = (block_index[None, :] <= query_index[:, None]) & (
            block_segs[None, :] == query_segs[:, None]
        )
        return jnp.where(allowed, raw_scores, masked_score)

    def max_pass(number, carry):
        top_score, total = carry
        start, key_three, value_three = block_keys(key_all, value_all, number)
        scores = block_scores(start, key_three)
        new_top = jnp.maximum(top_score, jnp.max(scores, axis=-1, keepdims=True))
        total = total * jnp.exp(top_score - new_top) + jnp.sum(
            jnp.exp(scores - new_top), axis=-1, keepdims=True
        )
        return (new_top, total)

    stat_shape = (KV_HEADS, groups, local_rows, 1)
    top_score, total = lax.fori_loop(
        low_block,
        high_block,
        max_pass,
        (jnp.full(stat_shape, masked_score, jnp.float32), jnp.zeros(stat_shape, jnp.float32)),
    )
    log_total = top_score + jnp.log(total)

    def mix_pass(number, mix_sum):
        start, key_three, value_three = block_keys(key_all, value_all, number)
        probs_low = jnp.exp(block_scores(start, key_three) - log_total).astype(jnp.bfloat16)
        return mix_sum + jnp.einsum(
            "kgts,skd->tkgd", probs_low, value_three, preferred_element_type=jnp.float32
        )

    mix_sum = lax.fori_loop(
        low_block,
        high_block,
        mix_pass,
        jnp.zeros((local_rows, KV_HEADS, groups, HEAD_DIM), jnp.float32),
    )
    attn_mix = mix_sum.reshape(local_rows, heads_width).astype(jnp.bfloat16)
    state = input_wide + jnp.dot(attn_mix, out_full, preferred_element_type=jnp.float32)
    root_two = inverse_root(state)
    normed_two = state * root_two
    gain_two = gain_two_full.astype(jnp.float32)
    moe_in = (normed_two * gain_two).astype(jnp.bfloat16)
    moe_group = lax.all_gather(moe_in, "dp", axis=0, tiled=True)
    expert_rows = (
        jnp.dot(place_low, moe_group, preferred_element_type=jnp.float32)
        .astype(jnp.bfloat16)
        .reshape(owned, rows_each, model_width)
    )
    cot_rows = (
        jnp.dot(place_low, grads_group, preferred_element_type=jnp.float32)
        .astype(jnp.bfloat16)
        .reshape(owned, rows_each, model_width)
    )
    group_logits = jnp.dot(moe_group, router_full, preferred_element_type=jnp.float32)
    group_weights = expert_weights(group_logits, chosen_group)
    own_mask = (all_experts[None, :] == own_experts[:, None]).astype(jnp.float32)
    own_weights = jnp.sum(group_weights[None, :, :] * own_mask[:, None, :], axis=2)
    row_weights = jnp.sum(jnp.where(place, own_weights[:, None, :], 0.0), axis=2)[..., None]
    grad_rows = (row_weights * cot_rows.astype(jnp.float32)).astype(jnp.bfloat16)
    gate_up = jnp.einsum("ecd,edf->ecf", expert_rows, in_full, preferred_element_type=jnp.float32)
    gate_part = gate_up[..., :FF]
    up_part = gate_up[..., FF:]
    sigmoid_gate = jax.nn.sigmoid(gate_part)
    activated = (gate_part * sigmoid_gate * up_part).astype(jnp.bfloat16)
    expert_out = jnp.einsum(
        "ecf,efd->ecd", activated, down_full, preferred_element_type=jnp.float32
    ).astype(jnp.bfloat16)
    expert_wide = expert_out.astype(jnp.float32)
    weighted = (row_weights * expert_wide).astype(jnp.bfloat16)
    combined = lax.dot_general(
        place_low,
        weighted.reshape(owned * rows_each, model_width),
        (((0,), (0,)), ((), ())),
        preferred_element_type=jnp.float32,
    ).astype(jnp.bfloat16)
    mixed = lax.psum_scatter(combined, "dp", scatter_dimension=0, tiled=True)
    output = (state + mixed.astype(jnp.float32)).astype(jnp.bfloat16)
    out_wide = cotangent.astype(jnp.float32)
    grad_dots = jnp.sum(cot_rows.astype(jnp.float32) * expert_wide, axis=-1)
    own_dots = jnp.sum(jnp.where(place, grad_dots[:, :, None], 0.0), axis=1)
    dots_wide = jnp.sum(own_dots[:, :, None] * own_mask[:, None, :], axis=0)
    dots_high = lax.reduce_precision(dots_wide, 8, 7)
    dots_low = lax.reduce_precision(dots_wide - dots_high, 8, 7)
    act_grad = jnp.einsum("ecd,efd->ecf", grad_rows, down_full, preferred_element_type=jnp.float32)
    gate_grad = act_grad * up_part * sigmoid_gate * (1.0 + gate_part * (1.0 - sigmoid_gate))
    up_grad = act_grad * gate_part * sigmoid_gate
    gate_up_grad = jnp.concatenate([gate_grad, up_grad], axis=-1).astype(jnp.bfloat16)
    rows_grad = jnp.einsum(
        "ecf,edf->ecd", gate_up_grad, in_full, preferred_element_type=jnp.float32
    ).astype(jnp.bfloat16)
    rows_total = lax.dot_general(
        place_low,
        rows_grad.reshape(owned * rows_each, model_width),
        (((0,), (0,)), ((), ())),
        preferred_element_type=jnp.float32,
    )
    back_sum = reduce_shards(
        pad_columns([rows_total, dots_high, dots_low], model_width + 128)
        .astype(jnp.bfloat16)
        .reshape(dp_size, local_rows, model_width + 128),
        [("dp", b) for b in x_bits + z_bits],
        {"dp": 0},
    )[0]
    in_total = jnp.einsum(
        "ecd,ecf->edf", expert_rows, gate_up_grad, preferred_element_type=jnp.float32
    ).astype(jnp.bfloat16)
    down_total = jnp.einsum(
        "ecf,ecd->efd", activated, grad_rows, preferred_element_type=jnp.float32
    ).astype(jnp.bfloat16)
    seq_stages = [("seq", b) for b in seq_bits]
    seq_size = lax.axis_size("seq")
    in_shard = reduce_shards(
        in_total.reshape(owned, seq_size, model_width // seq_size, 2 * FF), seq_stages, {"seq": 1}
    )[:, 0]
    down_cut = model_width // seq_size
    down_stack = jnp.stack(
        [down_total[:, :, i * down_cut : (i + 1) * down_cut] for i in range(seq_size)]
    )
    down_shard = reduce_shards(down_stack, seq_stages, {"seq": 0})[0]
    chosen = jnp.any(tok_routes[:, :, None] == all_experts, axis=1)
    logits = jnp.dot(moe_in, router_full, preferred_element_type=jnp.float32)
    route_weights = expert_weights(logits, chosen)
    weight_grad = (
        back_sum[:, model_width : model_width + EXPERTS]
        + back_sum[:, model_width + EXPERTS : model_width + 2 * EXPERTS]
    )
    logit_grad = route_weights * (
        weight_grad - jnp.sum(route_weights * weight_grad, axis=-1, keepdims=True)
    )
    router_total = jnp.dot(
        moe_in.astype(jnp.float32).T, logit_grad, precision=lax.Precision.HIGHEST
    )
    moe_in_grad = back_sum[:, :model_width] + jnp.dot(
        logit_grad, router_full.astype(jnp.float32).T, precision=lax.Precision.HIGHEST
    )
    gain_two_total = jnp.sum(moe_in_grad * normed_two, axis=0)
    normed_two_grad = moe_in_grad * gain_two_full.astype(jnp.float32)
    state_grad = out_wide + root_two * (
        normed_two_grad
        - normed_two * jnp.mean(normed_two_grad * normed_two, axis=-1, keepdims=True)
    )
    state_low = state_grad.astype(jnp.bfloat16)
    out_total = jnp.dot(attn_mix.T, state_low, preferred_element_type=jnp.float32)
    both_sizes = (dp_size, seq_size, model_width // (dp_size * seq_size))
    core_stage = [("seq", b) for b in seq_bits[:1]]
    y_stages = [("seq", b) for b in seq_bits[:0:-1]]
    x_stages = [("dp", b) for b in x_bits]
    z_stages = [("dp", b) for b in z_bits]
    second_shard = reduce_shards(
        pad_columns([out_total, router_total, gain_two_total[:, None]], out_width + 128)
        .astype(jnp.bfloat16)
        .reshape(both_sizes + (out_width + 128,)),
        core_stage + x_stages + y_stages + z_stages,
        {"dp": 0, "seq": 1},
    )[0, 0]
    out_shard = second_shard[:, :out_width]
    router_shard = second_shard[:, out_width : out_width + EXPERTS]
    gain_two_shard = second_shard[:, out_width + EXPERTS]
    mix_grad = (
        jnp.dot(state_low, out_full.T, preferred_element_type=jnp.float32)
        .astype(jnp.bfloat16)
        .reshape(local_rows, KV_HEADS, groups, HEAD_DIM)
    )
    row_delta = jnp.sum(
        mix_grad.astype(jnp.float32)
        * attn_mix.astype(jnp.float32).reshape(local_rows, KV_HEADS, groups, HEAD_DIM),
        axis=-1,
    )
    row_delta = jnp.transpose(row_delta, (1, 2, 0))[..., None]

    def grad_pass(number, carry):
        query_sum, key_buffer, value_buffer = carry
        start, key_three, value_three = block_keys(key_all, value_all, number)
        attn_probs = jnp.exp(block_scores(start, key_three) - log_total)
        probs_low = attn_probs.astype(jnp.bfloat16)
        raw_grad = jnp.einsum(
            "tkgd,skd->kgts", mix_grad, value_three, preferred_element_type=jnp.float32
        )
        scores_grad = (attn_probs * (raw_grad - row_delta) * score_scale).astype(jnp.bfloat16)
        query_sum = query_sum + jnp.einsum(
            "kgts,skd->tkgd", scores_grad, key_three, preferred_element_type=jnp.float32
        )
        key_piece = jnp.einsum(
            "kgts,tkgd->skd", scores_grad, grouped, preferred_element_type=jnp.float32
        ).reshape(key_block, kv_width)
        value_piece = jnp.einsum(
            "kgts,tkgd->skd", probs_low, mix_grad, preferred_element_type=jnp.float32
        ).reshape(key_block, kv_width)
        key_buffer = lax.dynamic_update_slice_in_dim(key_buffer, key_piece, start, 0)
        value_buffer = lax.dynamic_update_slice_in_dim(value_buffer, value_piece, start, 0)
        return (query_sum, key_buffer, value_buffer)

    grad_start = (
        jnp.zeros((local_rows, KV_HEADS, groups, HEAD_DIM), jnp.float32),
        jnp.zeros((length, kv_width), jnp.float32),
        jnp.zeros((length, kv_width), jnp.float32),
    )
    query_sum, key_grad, value_grad = lax.fori_loop(low_block, high_block, grad_pass, grad_start)
    both_total = reduce_shards(
        jnp.concatenate([key_grad, value_grad], axis=1)
        .astype(jnp.bfloat16)
        .reshape(seq_size, local_rows, 2 * kv_width),
        seq_stages,
        {"seq": 0},
    )[0]
    key_total = both_total[:, :kv_width]
    value_total = both_total[:, kv_width:]
    query_grad = unrotate(query_sum.reshape(local_rows, HEADS, HEAD_DIM), cosine_table, sine_table)
    key_total = unrotate(
        key_total.reshape(local_rows, KV_HEADS, HEAD_DIM), cosine_table, sine_table
    )
    proj_grad = jnp.concatenate(
        [
            query_grad.reshape(local_rows, heads_width),
            key_total.reshape(local_rows, kv_width),
            value_total,
        ],
        axis=-1,
    ).astype(jnp.bfloat16)
    qkv_total = jnp.dot(attn_in.T, proj_grad, preferred_element_type=jnp.float32)
    attn_in_grad = jnp.dot(proj_grad, qkv_full.T, preferred_element_type=jnp.float32)
    gain_one_total = jnp.sum(attn_in_grad * normed_one, axis=0)
    normed_one_grad = attn_in_grad * gain_full.astype(jnp.float32)
    input_grad = state_grad + root_one * (
        normed_one_grad
        - normed_one * jnp.mean(normed_one_grad * normed_one, axis=-1, keepdims=True)
    )
    first_shard = reduce_shards(
        pad_columns([qkv_total, gain_one_total[:, None]], qkv_width + 128)
        .astype(jnp.bfloat16)
        .reshape(both_sizes + (qkv_width + 128,)),
        core_stage + y_stages + x_stages + z_stages,
        {"dp": 0, "seq": 1},
    )[0, 0]
    qkv_shard = first_shard[:, :qkv_width]
    gain_one_shard = first_shard[:, qkv_width]
    return (
        output[None],
        input_grad[None],
        gain_one_shard,
        qkv_shard,
        out_shard,
        gain_two_shard,
        router_shard,
        in_shard,
        down_shard,
    )


def solution(mesh):
    placed = (
        P("dp", "seq", None),
        P("dp", "seq", None),
        P("dp", None),
        P("dp", "seq", None),
        P(("dp", "seq")),
        P(("dp", "seq"), None),
        P(("dp", "seq"), None),
        P(("dp", "seq")),
        P(("dp", "seq"), None),
        P("dp", "seq", None),
        P("dp", None, "seq"),
    )
    return jax.shard_map(
        body,
        mesh=mesh,
        in_specs=placed,
        out_specs=(
            P("dp", "seq", None),
            P("dp", "seq", None),
            P(("dp", "seq")),
            P(("dp", "seq"), None),
            P(("dp", "seq"), None),
            P(("dp", "seq")),
            P(("dp", "seq"), None),
            P("dp", "seq", None),
            P("dp", None, "seq"),
        ),
        check_vma=False,
    )
```

```python
import jax
import jax.numpy as jnp
from jax import lax
from jax.sharding import PartitionSpec as P

HEADS = 16
KV_HEADS = 8
HEAD_DIM = 64
EXPERTS = 32
FF = 512
TOP = 8
CAP = 34


epsilon = 1e-05
score_scale = 0.125
masked_score = -1e30
theta_base = 10000.0


def inverse_root(values):
    return lax.rsqrt(jnp.mean(values * values, axis=-1, keepdims=True) + epsilon)


def rope_tables(positions):
    half_dim = HEAD_DIM // 2
    frequencies = theta_base ** (-2.0 * jnp.arange(half_dim, dtype=jnp.float32) / HEAD_DIM)
    angles = positions.astype(jnp.float32)[:, None] * frequencies[None, :]
    return (jnp.cos(angles)[:, None, :], jnp.sin(angles)[:, None, :])


def rotate(values, cosine_table, sine_table):
    half_dim = HEAD_DIM // 2
    first_half = values[..., :half_dim]
    second_half = values[..., half_dim:]
    return jnp.concatenate(
        [
            first_half * cosine_table - second_half * sine_table,
            second_half * cosine_table + first_half * sine_table,
        ],
        axis=-1,
    )


def unrotate(values, cosine_table, sine_table):
    half_dim = HEAD_DIM // 2
    first_half = values[..., :half_dim]
    second_half = values[..., half_dim:]
    return jnp.concatenate(
        [
            first_half * cosine_table + second_half * sine_table,
            second_half * cosine_table - first_half * sine_table,
        ],
        axis=-1,
    )


def doc_positions(query_segs, all_segs, first_index):
    earlier = jnp.sum((all_segs[None, :] < query_segs[:, None]).astype(jnp.int32), axis=1)
    return first_index + jnp.arange(query_segs.shape[0], dtype=jnp.int32) - earlier


def swap(values, axis, bit):
    size = lax.axis_size(axis)
    return lax.ppermute(values, axis, [(i, i ^ bit) for i in range(size)])


def axis_bits(axis):
    bits = []
    bit = 1
    while bit < lax.axis_size(axis):
        bits.append(bit)
        bit *= 2
    return bits


def gather_shards(shard, axis, dim):
    index = lax.axis_index(axis)
    bits = axis_bits(axis)
    pieces = {0: shard}
    for bit in bits[1:] + bits[:1]:
        mine_high = (index & bit) != 0
        grown = {}
        for place, piece in pieces.items():
            other = swap(piece, axis, bit)
            grown[place] = jnp.where(mine_high, other, piece)
            grown[place | bit] = jnp.where(mine_high, piece, other)
        pieces = grown
    return jnp.concatenate([pieces[i] for i in range(len(pieces))], axis=dim)


def reduce_shards(partial, stages, dims):
    value = partial
    sizes = {axis: axis_bits(axis) for axis in dims}
    for number, (axis, bit) in enumerate(stages):
        dim = dims[axis]
        left = sizes[axis]
        at = left.index(bit)
        high = 2 ** (len(left) - 1 - at)
        low = 2**at
        shape = value.shape
        split = value.reshape(shape[:dim] + (high, 2, low) + shape[dim + 1 :])
        mine = jnp.where((lax.axis_index(axis) & bit) != 0, 1, 0)
        keep = lax.dynamic_index_in_dim(split, mine, dim + 1, keepdims=False)
        send = lax.dynamic_index_in_dim(split, 1 - mine, dim + 1, keepdims=False)
        got = swap(send.astype(jnp.bfloat16), axis, bit)
        value = keep.astype(jnp.float32) + got.astype(jnp.float32)
        value = value.reshape(shape[:dim] + (high * low,) + shape[dim + 1 :])
        sizes[axis] = left[:at] + left[at + 1 :]
        if number + 1 < len(stages):
            value = value.astype(jnp.bfloat16)
    return value


def expert_weights(logits, chosen):
    top = jnp.max(jnp.where(chosen, logits, -jnp.inf), axis=-1, keepdims=True)
    raised = jnp.where(chosen, jnp.exp(jnp.where(chosen, logits - top, 0.0)), 0.0)
    return raised / jnp.sum(raised, axis=-1, keepdims=True)


def pad_columns(arrays, width):
    rows = arrays[0].shape[0]
    used = sum(a.shape[1] for a in arrays)
    return jnp.concatenate(
        list(arrays) + [jnp.zeros((rows, width - used), arrays[0].dtype)], axis=1
    )


def body(
    block_input, out_grad, segments, routes, gain_attn, w_qkv, w_out, gain_moe, router, w_in, w_down
):
    tokens = block_input[0]
    cotangent = out_grad[0]
    seg_ids = segments[0]
    tok_routes = routes[0]
    local_rows = tokens.shape[0]
    model_width = tokens.shape[1]
    length = seg_ids.shape[0]
    heads_width = HEADS * HEAD_DIM
    kv_width = KV_HEADS * HEAD_DIM
    groups = HEADS // KV_HEADS
    key_block = min(length, 256)
    first_row = lax.axis_index("seq") * local_rows
    qkv_width = w_qkv.shape[1]
    out_width = w_out.shape[1]
    dp_size = lax.axis_size("dp")
    dp_index = lax.axis_index("dp")
    owned = EXPERTS // dp_size
    rows_each = dp_size * CAP
    group_rows = dp_size * local_rows
    dp_bits = axis_bits("dp")
    seq_bits = axis_bits("seq")
    x_bits = dp_bits[:1]
    z_bits = dp_bits[:0:-1]
    first_dense = lax.all_gather(
        pad_columns([w_qkv, gain_attn[:, None]], qkv_width + 128),
        ("dp", "seq"), axis=0, tiled=True,
    )
    qkv_full = first_dense[:, :qkv_width]
    gain_full = first_dense[:, qkv_width]
    second_dense = lax.all_gather(
        pad_columns([w_out, router, gain_moe[:, None]], out_width + 128),
        ("dp", "seq"), axis=0, tiled=True,
    )
    out_full = second_dense[:, :out_width]
    router_full = second_dense[:, out_width : out_width + EXPERTS]
    gain_two_full = second_dense[:, out_width + EXPERTS]
    grads_group = gather_shards(
        pad_columns([cotangent, tok_routes.astype(jnp.bfloat16)], model_width + 128), "dp", 0
    )
    routes_group = grads_group[:, model_width : model_width + TOP].astype(jnp.int32)
    grads_group = grads_group[:, :model_width]
    in_full = gather_shards(w_in, "seq", 1)
    down_full = gather_shards(w_down, "seq", 2)
    all_experts = jnp.arange(EXPERTS, dtype=jnp.int32)
    chosen_group = jnp.any(routes_group[:, :, None] == all_experts, axis=1)
    own_experts = dp_index * owned + jnp.arange(owned, dtype=jnp.int32)
    chosen_own = jnp.any(routes_group[None, :, :] == own_experts[:, None, None], axis=2)
    row_index = jnp.arange(group_rows, dtype=jnp.int32)
    upper = (row_index[:, None] <= row_index[None, :]).astype(jnp.bfloat16)
    slot_rank = (
        jnp.dot(chosen_own.astype(jnp.bfloat16), upper, preferred_element_type=jnp.float32)
        .astype(jnp.int32)
        - 1
    )
    slot_rank = jnp.where(chosen_own, slot_rank, -1)
    place = slot_rank[:, None, :] == jnp.arange(rows_each, dtype=jnp.int32)[None, :, None]
    place_low = place.astype(jnp.bfloat16).reshape(owned * rows_each, group_rows)
    input_wide = tokens.astype(jnp.float32)
    root_one = inverse_root(input_wide)
    normed_one = input_wide * root_one
    gain_one = gain_full.astype(jnp.float32)
    attn_in = (normed_one * gain_one).astype(jnp.bfloat16)
    projected = jnp.dot(attn_in, qkv_full, preferred_element_type=jnp.float32)
    query_segs = lax.dynamic_slice_in_dim(seg_ids, first_row, local_rows)
    positions = doc_positions(query_segs, seg_ids, first_row)
    cosine_table, sine_table = rope_tables(positions)
    queries = rotate(
        projected[:, :heads_width].reshape(local_rows, HEADS, HEAD_DIM), cosine_table, sine_table
    ).astype(jnp.bfloat16)
    key_local = (
        rotate(
            projected[:, heads_width : heads_width + kv_width].reshape(
                local_rows, KV_HEADS, HEAD_DIM
            ),
            cosine_table,
            sine_table,
        )
        .astype(jnp.bfloat16)
        .reshape(local_rows, kv_width)
    )
    value_local = projected[:, heads_width + kv_width :].astype(jnp.bfloat16)
    both_all = gather_shards(jnp.concatenate([key_local, value_local], axis=1), "seq", 0)
    key_all = both_all[:, :kv_width]
    value_all = both_all[:, kv_width:]
    grouped = queries.reshape(local_rows, KV_HEADS, groups, HEAD_DIM)
    query_index = first_row + jnp.arange(local_rows, dtype=jnp.int32)
    doc_start = jnp.sum((seg_ids < query_segs[0]).astype(jnp.int32))
    low_block = doc_start // key_block
    high_block = (first_row + local_rows - 1) // key_block + 1

    def block_keys(keys_flat, values_flat, number):
        start = (number * key_block).astype(jnp.int32)
        key_three = lax.dynamic_slice_in_dim(keys_flat, start, key_block, 0).reshape(
            key_block, KV_HEADS, HEAD_DIM
        )
        value_three = lax.dynamic_slice_in_dim(values_flat, start, key_block, 0).reshape(
            key_block, KV_HEADS, HEAD_DIM
        )
        return (start, key_three, value_three)

    def block_scores(start, key_three):
        raw_scores = (
            jnp.einsum("tkgd,skd->kgts", grouped, key_three, preferred_element_type=jnp.float32)
            * score_scale
        )
        block_index = start + jnp.arange(key_block, dtype=jnp.int32)
        block_segs = lax.dynamic_slice_in_dim(seg_ids, start, key_block)
        allowed = (block_index[None, :] <= query_index[:, None]) & (
            block_segs[None, :] == query_segs[:, None]
        )
        return jnp.where(allowed, raw_scores, masked_score)

    def max_pass(number, carry):
        top_score, total = carry
        start, key_three, value_three = block_keys(key_all, value_all, number)
        scores = block_scores(start, key_three)
        new_top = jnp.maximum(top_score, jnp.max(scores, axis=-1, keepdims=True))
        total = total * jnp.exp(top_score - new_top) + jnp.sum(
            jnp.exp(scores - new_top), axis=-1, keepdims=True
        )
        return (new_top, total)

    stat_shape = (KV_HEADS, groups, local_rows, 1)
    top_score, total = lax.fori_loop(
        low_block,
        high_block,
        max_pass,
        (jnp.full(stat_shape, masked_score, jnp.float32), jnp.zeros(stat_shape, jnp.float32)),
    )
    log_total = top_score + jnp.log(total)

    def mix_pass(number, mix_sum):
        start, key_three, value_three = block_keys(key_all, value_all, number)
        probs_low = jnp.exp(block_scores(start, key_three) - log_total).astype(jnp.bfloat16)
        return mix_sum + jnp.einsum(
            "kgts,skd->tkgd", probs_low, value_three, preferred_element_type=jnp.float32
        )

    mix_sum = lax.fori_loop(
        low_block,
        high_block,
        mix_pass,
        jnp.zeros((local_rows, KV_HEADS, groups, HEAD_DIM), jnp.float32),
    )
    attn_mix = mix_sum.reshape(local_rows, heads_width).astype(jnp.bfloat16)
    state = input_wide + jnp.dot(attn_mix, out_full, preferred_element_type=jnp.float32)
    root_two = inverse_root(state)
    normed_two = state * root_two
    gain_two = gain_two_full.astype(jnp.float32)
    moe_in = (normed_two * gain_two).astype(jnp.bfloat16)
    moe_group = lax.all_gather(moe_in, "dp", axis=0, tiled=True)
    expert_rows = (
        jnp.dot(place_low, moe_group, preferred_element_type=jnp.float32)
        .astype(jnp.bfloat16)
        .reshape(owned, rows_each, model_width)
    )
    cot_rows = (
        jnp.dot(place_low, grads_group, preferred_element_type=jnp.float32)
        .astype(jnp.bfloat16)
        .reshape(owned, rows_each, model_width)
    )
    group_logits = jnp.dot(moe_group, router_full, preferred_element_type=jnp.float32)
    group_weights = expert_weights(group_logits, chosen_group)
    own_mask = (all_experts[None, :] == own_experts[:, None]).astype(jnp.float32)
    own_weights = jnp.sum(group_weights[None, :, :] * own_mask[:, None, :], axis=2)
    row_weights = jnp.sum(jnp.where(place, own_weights[:, None, :], 0.0), axis=2)[..., None]
    grad_rows = (row_weights * cot_rows.astype(jnp.float32)).astype(jnp.bfloat16)
    gate_up = jnp.einsum("ecd,edf->ecf", expert_rows, in_full, preferred_element_type=jnp.float32)
    gate_part = gate_up[..., :FF]
    up_part = gate_up[..., FF:]
    sigmoid_gate = jax.nn.sigmoid(gate_part)
    activated = (gate_part * sigmoid_gate * up_part).astype(jnp.bfloat16)
    expert_out = jnp.einsum(
        "ecf,efd->ecd", activated, down_full, preferred_element_type=jnp.float32
    ).astype(jnp.bfloat16)
    expert_wide = expert_out.astype(jnp.float32)
    weighted = (row_weights * expert_wide).astype(jnp.bfloat16)
    combined = lax.dot_general(
        place_low,
        weighted.reshape(owned * rows_each, model_width),
        (((0,), (0,)), ((), ())),
        preferred_element_type=jnp.float32,
    ).astype(jnp.bfloat16)
    mixed = lax.psum_scatter(combined, "dp", scatter_dimension=0, tiled=True)
    output = (state + mixed.astype(jnp.float32)).astype(jnp.bfloat16)
    out_wide = cotangent.astype(jnp.float32)
    grad_dots = jnp.sum(cot_rows.astype(jnp.float32) * expert_wide, axis=-1)
    own_dots = jnp.sum(jnp.where(place, grad_dots[:, :, None], 0.0), axis=1)
    dots_wide = jnp.sum(own_dots[:, :, None] * own_mask[:, None, :], axis=0)
    dots_high = lax.reduce_precision(dots_wide, 8, 7)
    dots_low = lax.reduce_precision(dots_wide - dots_high, 8, 7)
    act_grad = jnp.einsum("ecd,efd->ecf", grad_rows, down_full, preferred_element_type=jnp.float32)
    gate_grad = act_grad * up_part * sigmoid_gate * (1.0 + gate_part * (1.0 - sigmoid_gate))
    up_grad = act_grad * gate_part * sigmoid_gate
    gate_up_grad = jnp.concatenate([gate_grad, up_grad], axis=-1).astype(jnp.bfloat16)
    rows_grad = jnp.einsum(
        "ecf,edf->ecd", gate_up_grad, in_full, preferred_element_type=jnp.float32
    ).astype(jnp.bfloat16)
    rows_total = lax.dot_general(
        place_low,
        rows_grad.reshape(owned * rows_each, model_width),
        (((0,), (0,)), ((), ())),
        preferred_element_type=jnp.float32,
    )
    back_sum = reduce_shards(
        pad_columns([rows_total, dots_high, dots_low], model_width + 128)
        .astype(jnp.bfloat16)
        .reshape(dp_size, local_rows, model_width + 128),
        [("dp", b) for b in x_bits + z_bits],
        {"dp": 0},
    )[0]
    in_total = jnp.einsum(
        "ecd,ecf->edf", expert_rows, gate_up_grad, preferred_element_type=jnp.float32
    ).astype(jnp.bfloat16)
    down_total = jnp.einsum(
        "ecf,ecd->efd", activated, grad_rows, preferred_element_type=jnp.float32
    ).astype(jnp.bfloat16)
    seq_stages = [("seq", b) for b in seq_bits]
    seq_size = lax.axis_size("seq")
    in_shard = reduce_shards(
        in_total.reshape(owned, seq_size, model_width // seq_size, 2 * FF), seq_stages, {"seq": 1}
    )[:, 0]
    down_cut = model_width // seq_size
    down_stack = jnp.stack(
        [down_total[:, :, i * down_cut : (i + 1) * down_cut] for i in range(seq_size)]
    )
    down_shard = reduce_shards(down_stack, seq_stages, {"seq": 0})[0]
    chosen = jnp.any(tok_routes[:, :, None] == all_experts, axis=1)
    logits = jnp.dot(moe_in, router_full, preferred_element_type=jnp.float32)
    route_weights = expert_weights(logits, chosen)
    weight_grad = (
        back_sum[:, model_width : model_width + EXPERTS]
        + back_sum[:, model_width + EXPERTS : model_width + 2 * EXPERTS]
    )
    logit_grad = route_weights * (
        weight_grad - jnp.sum(route_weights * weight_grad, axis=-1, keepdims=True)
    )
    router_total = jnp.dot(
        moe_in.astype(jnp.float32).T, logit_grad, precision=lax.Precision.HIGHEST
    )
    moe_in_grad = back_sum[:, :model_width] + jnp.dot(
        logit_grad, router_full.astype(jnp.float32).T, precision=lax.Precision.HIGHEST
    )
    gain_two_total = jnp.sum(moe_in_grad * normed_two, axis=0)
    normed_two_grad = moe_in_grad * gain_two_full.astype(jnp.float32)
    state_grad = out_wide + root_two * (
        normed_two_grad
        - normed_two * jnp.mean(normed_two_grad * normed_two, axis=-1, keepdims=True)
    )
    state_low = state_grad.astype(jnp.bfloat16)
    out_total = jnp.dot(attn_mix.T, state_low, preferred_element_type=jnp.float32)
    both_sizes = (dp_size, seq_size, model_width // (dp_size * seq_size))
    core_stage = [("seq", b) for b in seq_bits[:1]]
    y_stages = [("seq", b) for b in seq_bits[:0:-1]]
    x_stages = [("dp", b) for b in x_bits]
    z_stages = [("dp", b) for b in z_bits]
    second_shard = reduce_shards(
        pad_columns([out_total, router_total, gain_two_total[:, None]], out_width + 128)
        .astype(jnp.bfloat16)
        .reshape(both_sizes + (out_width + 128,)),
        core_stage + x_stages + y_stages + z_stages,
        {"dp": 0, "seq": 1},
    )[0, 0]
    out_shard = second_shard[:, :out_width]
    router_shard = second_shard[:, out_width : out_width + EXPERTS]
    gain_two_shard = second_shard[:, out_width + EXPERTS]
    mix_grad = (
        jnp.dot(state_low, out_full.T, preferred_element_type=jnp.float32)
        .astype(jnp.bfloat16)
        .reshape(local_rows, KV_HEADS, groups, HEAD_DIM)
    )
    row_delta = jnp.sum(
        mix_grad.astype(jnp.float32)
        * attn_mix.astype(jnp.float32).reshape(local_rows, KV_HEADS, groups, HEAD_DIM),
        axis=-1,
    )
    row_delta = jnp.transpose(row_delta, (1, 2, 0))[..., None]

    def grad_pass(number, carry):
        query_sum, key_buffer, value_buffer = carry
        start, key_three, value_three = block_keys(key_all, value_all, number)
        attn_probs = jnp.exp(block_scores(start, key_three) - log_total)
        probs_low = attn_probs.astype(jnp.bfloat16)
        raw_grad = jnp.einsum(
            "tkgd,skd->kgts", mix_grad, value_three, preferred_element_type=jnp.float32
        )
        scores_grad = (attn_probs * (raw_grad - row_delta) * score_scale).astype(jnp.bfloat16)
        query_sum = query_sum + jnp.einsum(
            "kgts,skd->tkgd", scores_grad, key_three, preferred_element_type=jnp.float32
        )
        key_piece = jnp.einsum(
            "kgts,tkgd->skd", scores_grad, grouped, preferred_element_type=jnp.float32
        ).reshape(key_block, kv_width)
        value_piece = jnp.einsum(
            "kgts,tkgd->skd", probs_low, mix_grad, preferred_element_type=jnp.float32
        ).reshape(key_block, kv_width)
        key_buffer = lax.dynamic_update_slice_in_dim(key_buffer, key_piece, start, 0)
        value_buffer = lax.dynamic_update_slice_in_dim(value_buffer, value_piece, start, 0)
        return (query_sum, key_buffer, value_buffer)

    grad_start = (
        jnp.zeros((local_rows, KV_HEADS, groups, HEAD_DIM), jnp.float32),
        jnp.zeros((length, kv_width), jnp.float32),
        jnp.zeros((length, kv_width), jnp.float32),
    )
    query_sum, key_grad, value_grad = lax.fori_loop(low_block, high_block, grad_pass, grad_start)
    both_total = reduce_shards(
        jnp.concatenate([key_grad, value_grad], axis=1)
        .astype(jnp.bfloat16)
        .reshape(seq_size, local_rows, 2 * kv_width),
        seq_stages,
        {"seq": 0},
    )[0]
    key_total = both_total[:, :kv_width]
    value_total = both_total[:, kv_width:]
    query_grad = unrotate(query_sum.reshape(local_rows, HEADS, HEAD_DIM), cosine_table, sine_table)
    key_total = unrotate(
        key_total.reshape(local_rows, KV_HEADS, HEAD_DIM), cosine_table, sine_table
    )
    proj_grad = jnp.concatenate(
        [
            query_grad.reshape(local_rows, heads_width),
            key_total.reshape(local_rows, kv_width),
            value_total,
        ],
        axis=-1,
    ).astype(jnp.bfloat16)
    query_low = query_grad.reshape(local_rows, heads_width).astype(jnp.bfloat16)
    query_total = jnp.dot(attn_in.T, query_low, preferred_element_type=jnp.float32)
    query_shard = reduce_shards(
        query_total.astype(jnp.bfloat16).reshape(both_sizes + (heads_width,)),
        core_stage + x_stages + z_stages + y_stages,
        {"dp": 0, "seq": 1},
    )[0, 0]
    rest_total = jnp.dot(attn_in.T, proj_grad[:, heads_width:], preferred_element_type=jnp.float32)
    attn_in_grad = jnp.dot(proj_grad, qkv_full.T, preferred_element_type=jnp.float32)
    gain_one_total = jnp.sum(attn_in_grad * normed_one, axis=0)
    normed_one_grad = attn_in_grad * gain_full.astype(jnp.float32)
    input_grad = state_grad + root_one * (
        normed_one_grad
        - normed_one * jnp.mean(normed_one_grad * normed_one, axis=-1, keepdims=True)
    )
    rest_width = qkv_width - heads_width
    rest_shard = reduce_shards(
        pad_columns([rest_total, gain_one_total[:, None]], rest_width + 128)
        .astype(jnp.bfloat16)
        .reshape(both_sizes + (rest_width + 128,)),
        core_stage + y_stages + x_stages + z_stages,
        {"dp": 0, "seq": 1},
    )[0, 0]
    qkv_shard = jnp.concatenate([query_shard, rest_shard[:, :rest_width]], axis=1)
    gain_one_shard = rest_shard[:, rest_width]
    return (
        output[None],
        input_grad[None],
        gain_one_shard,
        qkv_shard,
        out_shard,
        gain_two_shard,
        router_shard,
        in_shard,
        down_shard,
    )


def solution(mesh):
    placed = (
        P("dp", "seq", None),
        P("dp", "seq", None),
        P("dp", None),
        P("dp", "seq", None),
        P(("dp", "seq")),
        P(("dp", "seq"), None),
        P(("dp", "seq"), None),
        P(("dp", "seq")),
        P(("dp", "seq"), None),
        P("dp", "seq", None),
        P("dp", None, "seq"),
    )
    return jax.shard_map(
        body,
        mesh=mesh,
        in_specs=placed,
        out_specs=(
            P("dp", "seq", None),
            P("dp", "seq", None),
            P(("dp", "seq")),
            P(("dp", "seq"), None),
            P(("dp", "seq"), None),
            P(("dp", "seq")),
            P(("dp", "seq"), None),
            P("dp", "seq", None),
            P("dp", None, "seq"),
        ),
        check_vma=False,
    )
```
